32 devices in a mesh: grp: 4 (over y, x), exp: 8 (over z, core).
Axes of the slice: x: 2, y: 2, z: 4, core: 2. Of those that a mesh axis runs over, the one named last changes fastest.
Arguments:
- tokens: bfloat16 [4096, 2048], P(('grp', 'exp')), may hold values from -6 to 6
- cotangent: bfloat16 [4096, 2048], P(('grp', 'exp')), may hold values from -3 to 3
- timestep: int32 [4096], P(('grp', 'exp')), may hold values from 0 to 15
- shift_table: float32 [16, 2048], replicated, may hold values from -3 to 3
- scale_table: float32 [16, 2048], replicated, may hold values from -2.5 to 2.5
- gate_table: float32 [16, 2048], replicated, may hold values from -4 to 4
- chosen: int32 [4, 4, 256], P('grp'), may hold values from 0 to 1023, as said below
- combine: float32 [4, 4, 256], P('grp'), may hold values from 0.1 to 1
- w_gate: bfloat16 [8, 704, 2048], P('exp'), may hold values from -0.125 to 0.125
- w_up: bfloat16 [8, 704, 2048], P('exp'), may hold values from -0.125 to 0.125
- w_down: bfloat16 [8, 704, 2048], P('exp'), may hold values from -0.15625 to 0.15625
Outputs:
- d_tokens: bfloat16 [4096, 2048], P(('grp', 'exp'))
- d_combine: float32 [4, 8, 128], P('grp', 'exp')
- d_w_gate: bfloat16 [8, 704, 2048], P('exp', None, 'grp')
- d_w_up: bfloat16 [8, 704, 2048], P('exp', None, 'grp')
- d_w_down: bfloat16 [8, 704, 2048], P('exp', None, 'grp')
The draws below stay inside these ranges and needn't reach their ends.
Inputs may be any that keep to these rules, and one draw needn't show every extreme that they name: Each list chosen[g, e, :] names 256 different tokens of group g; at most 64 of them lie among the 128 tokens of one device, and in every list some device's tokens supply exactly 64.
All inputs are finite; a program needn't handle non-finite values.
Results may differ from the reference program's by a relative error of at most 0.014.
Values may be sent and summed in bfloat16 or wider, within the bound.
No kernel may reach another device: no remote copies, remote signals or barrier semaphores. Data moves between devices by JAX's collectives and lax.ppermute only.
A program may use at most 128 MiB of HBM per device.

```python
import math
import jax
import jax.numpy as jnp
from jax import lax

D = 2048
FF = 1408
TSTEPS = 16
TOK_DEV = 128
GROUPS = 4
PEERS = 8
EXPERTS = 4
FF_HALF = 704
CAP = 256
SLOT = 64
TOKENS = 4096


def pick_order(sub_key):
    return jax.random.permutation(sub_key, TOK_DEV)


def one_list(list_key):
    owner_key, shift_key, pick_key, mix_key = jax.random.split(list_key, 4)
    half_slot = SLOT // 2
    owner_order = jax.random.permutation(owner_key, PEERS)
    moved_rows = jax.random.randint(shift_key, (PEERS // 2,), 0, half_slot + 1)
    moved_rows = moved_rows.at[0].set(half_slot)
    paired = jnp.stack([half_slot + moved_rows, half_slot - moved_rows], axis=1).reshape(PEERS)
    counts = jnp.zeros((PEERS,), jnp.int32).at[owner_order].set(paired.astype(jnp.int32))
    pick_keys = jax.random.split(pick_key, PEERS)
    picked = jax.vmap(pick_order)(pick_keys)[:, :SLOT].astype(jnp.int32)
    token_ids = picked + jnp.arange(PEERS, dtype=jnp.int32)[:, None] * TOK_DEV
    is_valid = jnp.arange(SLOT, dtype=jnp.int32)[None, :] < counts[:, None]
    scores = jnp.where(is_valid, 0, 1).reshape(-1) * (PEERS * SLOT) + jnp.arange(PEERS * SLOT, dtype=jnp.int32)
    ordering = jnp.argsort(scores, stable=True)[:CAP]
    chosen_ids = token_ids.reshape(-1)[ordering]
    return chosen_ids[jax.random.permutation(mix_key, CAP)]


def draw_chosen(key, part):
    base_key = jax.random.fold_in(key, 17)
    list_keys = jax.random.split(base_key, GROUPS * EXPERTS)
    all_lists = jax.vmap(one_list)(list_keys)
    return all_lists.reshape(GROUPS, EXPERTS, CAP).astype(jnp.int32)


def plant(entries, own_key, smallest, high):
    longest = entries.shape.index(max(entries.shape))
    spots = []
    for shift in (0, 1):
        where = [jax.random.randint(jax.random.fold_in(own_key, axis), (), 0, length) for axis, length in enumerate(entries.shape)]
        where[longest] = (where[longest] + shift) % entries.shape[longest]
        spots.append(tuple(where))
    return entries.at[spots[0]].set(smallest).at[spots[1]].set(high)


def block_levels(rng, shape, pieces, least, largest):
    factor_of, own = 1.0, jax.random.fold_in(rng, 6)
    for axis_at, shards_of in pieces:
        heights = jnp.exp(jax.random.uniform(jax.random.fold_in(own, axis_at), (shards_of,), jnp.float32, least / len(pieces), largest / len(pieces)))
        factor_of = factor_of * jnp.repeat(heights, shape[axis_at] // shards_of).reshape([-1 if axis == axis_at else 1 for axis in range(len(shape))])
    return factor_of


def scatter_about(own_key, dims, spread, reach, cuts=(), kind=jnp.bfloat16):
    drawn = jax.random.normal(own_key, dims, jnp.float32) * spread
    if len(cuts) > 0:
        drawn = block_levels(own_key, dims, cuts, -0.22, 0.18) * drawn
    return jnp.clip(drawn, min=-reach, max=reach).astype(kind)


def setup_inputs(seed: int = 0) -> dict:
    seeds = jax.random.split(jax.random.key(seed), 12)
    tokens = scatter_about(seeds[0], (TOKENS, D), 1.0, 6.0, ((0, 32),))
    cotangent = scatter_about(seeds[1], (TOKENS, D), 0.5, 3.0, ((0, 32),))
    timestep = plant(jax.random.randint(seeds[2], (TOKENS,), 0, TSTEPS), jax.random.fold_in(seeds[2], 1), 0, TSTEPS - 1).astype(jnp.int32)
    shift_table = scatter_about(seeds[3], (TSTEPS, D), 0.5, 3.0, (), jnp.float32)
    scale_table = scatter_about(seeds[4], (TSTEPS, D), 0.3, 2.5, (), jnp.float32)
    gate_table = scatter_about(seeds[5], (TSTEPS, D), 1.0, 4.0, (), jnp.float32)
    chosen = draw_chosen(jax.random.fold_in(seeds[11], 71), 0)
    combine = jnp.clip(jnp.exp(math.log(1.0) - 2.3025851 * jax.random.uniform(seeds[7], (GROUPS, EXPERTS, CAP), jnp.float32) ** block_levels(seeds[7], (GROUPS, EXPERTS, CAP), ((0, 4),), -0.2, 0.2)), 0.1, 1.0)
    w_gate = scatter_about(seeds[8], (PEERS, FF_HALF, D), D ** -0.5, 0.125, ((0, 8),))
    w_up = scatter_about(seeds[9], (PEERS, FF_HALF, D), D ** -0.5, 0.125, ((0, 8),))
    w_down = scatter_about(seeds[10], (PEERS, FF_HALF, D), FF ** -0.5, 0.15625, ((0, 8),))
    return dict(tokens=tokens, cotangent=cotangent, timestep=timestep, shift_table=shift_table, scale_table=scale_table, gate_table=gate_table, chosen=chosen, combine=combine, w_gate=w_gate, w_up=w_up, w_down=w_down)


EPSILON = 1e-06

def layer_stats(group_x):
    values = group_x.astype(jnp.float32)
    centred = values - lax.optimization_barrier(jnp.mean(values, axis=1, keepdims=True))
    inverse = lax.rsqrt(lax.optimization_barrier(jnp.mean(centred * centred, axis=1, keepdims=True)) + EPSILON)
    return (centred * inverse, inverse)

def reference(tokens, cotangent, timestep, shift_table, scale_table, gate_table, chosen, combine, w_gate, w_up, w_down):
    groups = chosen.shape[0]
    experts = chosen.shape[1]
    capacity = chosen.shape[2]
    half_units = w_gate.shape[1]
    features = tokens.shape[1]
    group_tokens = tokens.shape[0] // groups
    gate_split = w_gate.reshape(experts, 2, half_units, features)
    up_split = w_up.reshape(experts, 2, half_units, features)
    down_split = w_down.reshape(experts, 2, half_units, features)

    def one_group(grad_sums, group_inputs):
        group_x, group_cot, group_steps, group_lists, group_weights = group_inputs
        normed, inverse = layer_stats(group_x)
        scale_rows = scale_table[group_steps]
        modulated = (normed * (1.0 + scale_rows) + shift_table[group_steps]).astype(jnp.bfloat16)
        scaled = (gate_table[group_steps] * group_cot.astype(jnp.float32)).astype(jnp.bfloat16)

        def one_expert(d_modulated, expert_inputs):
            rows, row_weight, gate_pair, up_pair, down_pair = expert_inputs
            rows_in = jnp.take(modulated, rows, axis=0)
            rows_grad = jnp.take(scaled, rows, axis=0)
            pre_gates = []
            pre_ups = []
            hiddens = []
            expert_out = jnp.zeros((capacity, features), jnp.float32)
            for half_index in range(2):
                pre_gate = jnp.dot(rows_in, gate_pair[half_index].T, preferred_element_type=jnp.float32)
                pre_up = jnp.dot(rows_in, up_pair[half_index].T, preferred_element_type=jnp.float32)
                hidden = (pre_gate * jax.nn.sigmoid(pre_gate) * pre_up).astype(jnp.bfloat16)
                expert_out = expert_out + jnp.dot(hidden, down_pair[half_index], preferred_element_type=jnp.float32)
                pre_gates.append(pre_gate)
                pre_ups.append(pre_up)
                hiddens.append(hidden)
            inner = lax.optimization_barrier(jnp.sum(rows_grad.astype(jnp.float32) * expert_out, axis=1))
            d_out = (row_weight[:, None] * rows_grad.astype(jnp.float32)).astype(jnp.bfloat16)
            grads_gate = []
            grads_up = []
            grads_down = []
            part_sum = jnp.zeros((capacity, features), jnp.float32)
            for half_index in range(2):
                pre_gate = pre_gates[half_index]
                sigmoid_gate = jax.nn.sigmoid(pre_gate)
                d_hidden = jnp.dot(d_out, down_pair[half_index].T, preferred_element_type=jnp.float32)
                grads_down.append(jnp.dot(hiddens[half_index].T, d_out, preferred_element_type=jnp.float32).astype(jnp.bfloat16))
                d_gate = (d_hidden * pre_ups[half_index] * sigmoid_gate * (1.0 + pre_gate * (1.0 - sigmoid_gate))).astype(jnp.bfloat16)
                d_up = (d_hidden * (pre_gate * sigmoid_gate)).astype(jnp.bfloat16)
                grads_gate.append(jnp.dot(d_gate.T, rows_in, preferred_element_type=jnp.float32).astype(jnp.bfloat16))
                grads_up.append(jnp.dot(d_up.T, rows_in, preferred_element_type=jnp.float32).astype(jnp.bfloat16))
                part_sum = part_sum + jnp.dot(d_gate, gate_pair[half_index], preferred_element_type=jnp.float32) + jnp.dot(d_up, up_pair[half_index], preferred_element_type=jnp.float32)
            part_rows = part_sum.astype(jnp.bfloat16)
            d_modulated = d_modulated.at[rows].add(part_rows.astype(jnp.float32))
            return (d_modulated, (inner, jnp.stack(grads_gate), jnp.stack(grads_up), jnp.stack(grads_down)))
        start = jnp.zeros((group_tokens, features), jnp.float32)
        d_modulated, (inners, grad_g, grad_u, grad_d) = lax.scan(one_expert, start, (group_lists, group_weights, gate_split, up_split, down_split))
        d_normed = d_modulated * (1.0 + scale_rows)
        d_x = inverse * (d_normed - lax.optimization_barrier(jnp.mean(d_normed, axis=1, keepdims=True)) - normed * lax.optimization_barrier(jnp.mean(d_normed * normed, axis=1, keepdims=True)))
        new_sums = (grad_sums[0] + grad_g.astype(jnp.float32), grad_sums[1] + grad_u.astype(jnp.float32), grad_sums[2] + grad_d.astype(jnp.float32))
        return (new_sums, (d_x.astype(jnp.bfloat16), inners))
    zero_grad = jnp.zeros((experts, 2, half_units, features), jnp.float32)
    grad_sums, (d_tokens, inners) = lax.scan(one_group, (zero_grad, zero_grad, zero_grad), (tokens.reshape(groups, group_tokens, features), cotangent.reshape(groups, group_tokens, features), timestep.reshape(groups, group_tokens), chosen, combine))
    d_tokens = d_tokens.reshape(groups * group_tokens, features)
    d_combine = inners.reshape(groups, experts * 2, capacity // 2)
    d_w_gate = (grad_sums[0] / groups).astype(jnp.bfloat16).reshape(experts * 2, half_units, features)
    d_w_up = (grad_sums[1] / groups).astype(jnp.bfloat16).reshape(experts * 2, half_units, features)
    d_w_down = (grad_sums[2] / groups).astype(jnp.bfloat16).reshape(experts * 2, half_units, features)
    return (d_tokens, d_combine, d_w_gate, d_w_up, d_w_down)
```

```python
import functools

import jax
import jax.numpy as jnp
from jax import lax
from jax.experimental import pallas as pl
from jax.experimental.pallas import tpu as pltpu
from jax.sharding import PartitionSpec as P

EPSILON = 1e-06
F32 = jnp.float32
BF16 = jnp.bfloat16
NN = (((1,), (0,)), ((), ()))
NT = (((1,), (1,)), ((), ()))
TN = (((0,), (0,)), ((), ()))


def dot(left, right, dims=NN):
    return lax.dot_general(left, right, dims, preferred_element_type=F32)


def swap(shard, axis, bits):
    return lax.ppermute(shard, axis, [(i, i ^ bits) for i in range(lax.axis_size(axis))])


def iota(shape, dim):
    return lax.broadcasted_iota(jnp.int32, shape, dim)


def call(body, outs, args, smem=0, scratch=(), flops=0, moved=0):
    spaces = [pltpu.SMEM] * smem + [pltpu.VMEM] * (len(args) - smem)
    return pl.pallas_call(
        body,
        out_shape=[jax.ShapeDtypeStruct(shape, dtype) for shape, dtype in outs],
        in_specs=[pl.BlockSpec(memory_space=space) for space in spaces],
        out_specs=[pl.BlockSpec(memory_space=pltpu.VMEM) for _ in outs],
        scratch_shapes=list(scratch),
        cost_estimate=pl.CostEstimate(flops=flops, bytes_accessed=moved, transcendentals=0),
    )(*args)


def table_rows(step_ref, table):
    classes = table.shape[0]
    tokens = step_ref.shape[1]
    picks = (iota((classes, tokens), 0) == step_ref[...]).astype(F32).T.astype(BF16)
    high = table.astype(BF16)
    rest = table - high.astype(F32)
    middle = rest.astype(BF16)
    low = (rest - middle.astype(F32)).astype(BF16)
    return dot(picks, high) + dot(picks, middle) + dot(picks, low)


def layer_stats(values):
    centred = values - jnp.mean(values, axis=1, keepdims=True)
    inverse = lax.rsqrt(jnp.mean(centred * centred, axis=1, keepdims=True) + EPSILON)
    return centred * inverse, inverse


def pick_kernel(slots, at_ref, tokens_ref, step_ref, shift_ref, scale_ref, chosen_ref, pick_ref, *out_refs):
    experts, capacity = chosen_ref.shape
    count = tokens_ref.shape[0]
    device = at_ref[0]
    here = device // 2
    ones = jnp.ones((8, capacity), BF16)
    earlier = (iota((count, count), 0) < iota((count, count), 1)).astype(BF16)
    for j in range(experts):
        wanted = chosen_ref[pl.ds(here ^ j, 1), :] - device * count
        named = (iota((count, capacity), 0) == wanted).astype(F32).astype(BF16)
        taken = dot(ones, named, NT)
        place = dot(taken.astype(BF16), earlier)
        match = (place[0:1].astype(jnp.int32) == iota((slots, count), 0)) & (taken[0:1] > 0.5)
        pick_ref[j * slots : (j + 1) * slots, :] = match.astype(F32).astype(BF16)
    normed, _ = layer_stats(tokens_ref[...].astype(F32))
    scale = table_rows(step_ref, scale_ref[...])
    shift = table_rows(step_ref, shift_ref[...])
    modulated = (normed * (1.0 + scale) + shift).astype(BF16)
    for j in range(experts):
        out_refs[j][...] = dot(pick_ref[j * slots : (j + 1) * slots, :], modulated).astype(BF16)


def grad_kernel(slots, cotangent_ref, step_ref, gate_ref, pick_ref, *out_refs):
    gate = table_rows(step_ref, gate_ref[...])
    scaled = (gate * cotangent_ref[...].astype(F32)).astype(BF16)
    for j in range(len(out_refs)):
        out_refs[j][...] = dot(pick_ref[j * slots : (j + 1) * slots, :], scaled).astype(BF16)


def place_kernel(count, slots, at_ref, chosen_ref, place_ref, back_ref):
    experts, capacity = chosen_ref.shape
    device = at_ref[0]
    here, core = device // 2, device % 2
    shift = count.bit_length() - 1
    row = chosen_ref[pl.ds(here, 1), :]
    across = jnp.broadcast_to(row, (capacity, capacity))
    down = across.astype(F32).T.astype(jnp.int32)

    def slot_of(tokens, ranks):
        owner = lax.shift_right_logical(tokens, shift)
        apart = lax.shift_right_logical(owner, 1) ^ here
        other = (owner & 1) ^ core
        return (other * experts + apart) * slots + ranks

    owner_across = lax.shift_right_logical(across, shift)
    owner_down = lax.shift_right_logical(down, shift)
    same = owner_across == owner_down
    rank_down = jnp.sum((same & (across < down)).astype(F32), axis=1, keepdims=True)
    rank_across = jnp.sum((same & (down < across)).astype(F32), axis=0, keepdims=True)
    slot_down = slot_of(down[:, 0:1], rank_down.astype(jnp.int32))
    slot_across = slot_of(row, rank_across.astype(jnp.int32))
    total = place_ref.shape[1]
    place_ref[...] = (iota((capacity, total), 1) == slot_down).astype(F32).astype(BF16)
    back_ref[...] = (iota((total, capacity), 0) == slot_across).astype(F32).astype(BF16)


def gather_rows(place_ref, block_refs, slot_ref):
    slots = block_refs[0].shape[0]
    for index, block in enumerate(block_refs):
        slot_ref[index * slots : (index + 1) * slots, :] = block[...]
    return dot(place_ref[...], slot_ref[...]).astype(BF16)


def put_slices(rows_ref, at_ref, own_ref, sent_refs):
    half = rows_ref.shape[0] // 2
    width = own_ref.shape[1]
    core, group = at_ref[0] % 2, at_ref[1]
    mine = pl.ds(pl.multiple_of(core * half, half), half)
    own_ref[...] = rows_ref[:, pl.ds(pl.multiple_of(group * width, width), width)]
    for j, sent in enumerate(sent_refs):
        start = pl.multiple_of((group ^ (j + 1)) * width, width)
        sent[...] = rows_ref[mine, pl.ds(start, width)]


def forward_kernel(blocks, groups, at_ref, *refs):
    block_refs = refs[:blocks]
    place_ref, combine_ref, gate_ref, up_ref = refs[blocks : blocks + 4]
    hidden_ref, own_ref = refs[blocks + 4 : blocks + 6]
    sent_refs = refs[blocks + 6 : blocks + 5 + groups]
    weighed_ref, into_gate_ref, into_up_ref = refs[blocks + 5 + groups : blocks + 8 + groups]
    slot_ref, rows_ref = refs[blocks + 8 + groups :]
    rows_ref[...] = gather_rows(place_ref, block_refs, slot_ref)
    put_slices(rows_ref, at_ref, own_ref, sent_refs)
    weight = combine_ref[pl.ds(at_ref[0] // 2, 1), :]
    rows = rows_ref[...]
    pre_gate = dot(gate_ref[...], rows, NT)
    pre_up = dot(up_ref[...], rows, NT)
    sigmoid = jax.nn.sigmoid(pre_gate)
    silu = pre_gate * sigmoid
    hidden = silu * pre_up
    hidden_ref[...] = hidden
    weighed_ref[...] = (weight * hidden).astype(BF16)
    into_gate_ref[...] = weight * pre_up * sigmoid * (1.0 + pre_gate * (1.0 - sigmoid))
    into_up_ref[...] = weight * silu


def backward_kernel(blocks, groups, at_ref, *refs):
    block_refs = refs[:blocks]
    place_ref, down_ref, hidden_ref, into_gate_ref, into_up_ref = refs[blocks : blocks + 5]
    grads_ref, inner_ref, own_ref = refs[blocks + 5 : blocks + 8]
    sent_refs = refs[blocks + 8 : blocks + 7 + groups]
    slot_ref, rows_ref = refs[blocks + 7 + groups :]
    half_units = down_ref.shape[0]
    rows_ref[...] = gather_rows(place_ref, block_refs, slot_ref)
    put_slices(rows_ref, at_ref, own_ref, sent_refs)
    raw = dot(down_ref[...], rows_ref[...], NT)
    grads_ref[:half_units, :] = (raw * into_gate_ref[...]).astype(BF16)
    grads_ref[half_units:, :] = (raw * into_up_ref[...]).astype(BF16)
    inner_ref[...] = jnp.sum(raw * hidden_ref[...], axis=0, keepdims=True)


def rows_kernel(grads_ref, gate_ref, up_ref, back_ref, rows_ref, other_ref):
    half_units = gate_ref.shape[0]
    total = dot(grads_ref[:half_units, :], gate_ref[...], TN)
    total += dot(grads_ref[half_units:, :], up_ref[...], TN)
    rows_ref[...] = total.astype(BF16)
    other_ref[...] = dot(back_ref[other_ref.shape[0] :, :], rows_ref[...]).astype(BF16)


def pair_kernel(at_ref, rows_ref, back_ref, other_ref, inner_ref, inner_other_ref, combine_ref, *out_refs):
    half = combine_ref.shape[1]
    slots = out_refs[0].shape[0]
    start = pl.ds(pl.multiple_of((at_ref[0] % 2) * half, half), half)
    combine_ref[...] = inner_ref[:, start] + inner_other_ref[:, start]
    for j, out in enumerate(out_refs):
        at = slice(j * slots, (j + 1) * slots)
        out[...] = (dot(back_ref[at, :], rows_ref[...]) + other_ref[at, :].astype(F32)).astype(BF16)


def final_kernel(tokens_ref, step_ref, scale_ref, pick_ref, *refs):
    block_refs, (out_ref, slot_ref) = refs[:-2], refs[-2:]
    slots = block_refs[0].shape[0]
    for j, block in enumerate(block_refs):
        slot_ref[j * slots : (j + 1) * slots, :] = block[...]
    d_modulated = dot(pick_ref[...], slot_ref[...], TN)
    normed, inverse = layer_stats(tokens_ref[...].astype(F32))
    d_normed = d_modulated * (1.0 + table_rows(step_ref, scale_ref[...]))
    out_ref[...] = (
        inverse
        * (
            d_normed
            - jnp.mean(d_normed, axis=1, keepdims=True)
            - normed * jnp.mean(d_normed * normed, axis=1, keepdims=True)
        )
    ).astype(BF16)


def weight_kernel(groups, outs, at_ref, *refs):
    own_ref = refs[0]
    mine_refs = refs[1:groups]
    other_refs = refs[groups : 2 * groups - 1]
    factor_refs = refs[2 * groups - 1 : 3 * groups - 1]
    out_refs = refs[3 * groups - 1 : 3 * groups - 1 + outs]
    rows_ref = refs[-1]
    capacity = own_ref.shape[0]
    half = capacity // 2
    core = at_ref[0] % 2
    rows_ref[0] = own_ref[...]
    for j in range(groups - 1):
        rows_ref[j + 1, pl.ds(pl.multiple_of(core * half, half), half), :] = mine_refs[j][...]
        rows_ref[j + 1, pl.ds(pl.multiple_of((1 - core) * half, half), half), :] = other_refs[j][...]
    units = out_refs[0].shape[1]
    for index, out in enumerate(out_refs):
        total = None
        for j in range(groups):
            part = dot(factor_refs[j][index * units : (index + 1) * units, :], rows_ref[j])
            total = part if total is None else total + part
        out[0] = (total / groups).astype(BF16)


def on_device(tokens, cotangent, timestep, shift_table, scale_table, gate_table, chosen, combine, w_gate, w_up, w_down):
    peers = lax.axis_size("exp")
    groups = lax.axis_size("grp")
    count, features = tokens.shape
    capacity = chosen.shape[2]
    experts = peers // 2
    slots = 2 * capacity // peers
    units = w_gate.shape[1]
    width = features // groups
    at = jnp.stack([lax.axis_index("exp"), lax.axis_index("grp")]).astype(jnp.int32)
    steps = timestep.reshape(1, count)
    lists, weights = chosen[0], combine[0]
    gate_half, up_half, down_half = w_gate[0], w_up[0], w_down[0]
    sent = [((slots, features), BF16)] * experts
    product = 2 * capacity * features * units

    def dispatch(parts):
        arrived = [parts[0]] + [swap(parts[j], "exp", 2 * j) for j in range(1, experts)]
        return arrived + [swap(part, "exp", 1) for part in arrived]

    picks, *rows_out = call(
        functools.partial(pick_kernel, slots),
        [((experts * slots, count), BF16)] + sent,
        (at, tokens, steps, shift_table, scale_table, lists),
        smem=1,
        flops=10**9,
        moved=2 * 10**6,
    )
    blocks_in = dispatch(rows_out)
    grads_out = call(
        functools.partial(grad_kernel, slots),
        sent,
        (cotangent, steps, gate_table, picks),
        flops=10**9,
        moved=2 * 10**6,
    )
    blocks_grad = dispatch(grads_out)
    place, back = call(
        functools.partial(place_kernel, count, slots),
        [((capacity, peers * slots), BF16), ((peers * slots, capacity), BF16)],
        (at, lists),
        smem=1,
        flops=10**8,
        moved=10**6,
    )
    slices = [((capacity, width), BF16)] + [((capacity // 2, width), BF16)] * (groups - 1)
    gather_scratch = [pltpu.VMEM((peers * slots, features), BF16), pltpu.VMEM((capacity, features), BF16)]
    hidden, own_in, *rest = call(
        functools.partial(forward_kernel, peers, groups),
        [((units, capacity), F32)] + slices + [((units, capacity), BF16)] + [((units, capacity), F32)] * 2,
        (at, *blocks_in, place, weights, gate_half, up_half),
        smem=1,
        scratch=gather_scratch,
        flops=3 * product,
        moved=12 * 10**6,
    )
    sent_in, (weighed, into_gate, into_up) = rest[: groups - 1], rest[groups - 1 :]
    grads, inner, own_grad, *sent_grad = call(
        functools.partial(backward_kernel, peers, groups),
        [((2 * units, capacity), BF16), ((1, capacity), F32)] + slices,
        (at, *blocks_grad, place, down_half, hidden, into_gate, into_up),
        smem=1,
        scratch=gather_scratch,
        flops=2 * product,
        moved=10 * 10**6,
    )
    d_rows, d_other = call(
        rows_kernel,
        [((capacity, features), BF16), ((capacity, features), BF16)],
        (grads, gate_half, up_half, back),
        flops=3 * product,
        moved=10 * 10**6,
    )
    d_combine, *d_out = call(
        pair_kernel,
        [((1, capacity // 2), F32)] + sent,
        (at, d_rows, back, swap(d_other, "exp", 1), inner, swap(inner, "exp", 1)),
        smem=1,
        flops=product // 2,
        moved=4 * 10**6,
    )
    returned = [d_out[0]] + [swap(d_out[j], "exp", 2 * j) for j in range(1, experts)]
    (d_tokens,) = call(
        final_kernel,
        [((count, features), BF16)],
        (tokens, steps, scale_table, picks, *returned),
        scratch=[pltpu.VMEM((experts * slots, features), BF16)],
        flops=10**9,
        moved=2 * 10**6,
    )

    def across(part):
        return [swap(part, "grp", j) for j in range(1, groups)]

    def weight_grads(own, sends, factor, outs):
        mine = [swap(part, "grp", j + 1) for j, part in enumerate(sends)]
        others = [swap(part, "exp", 1) for part in mine]
        return call(
            functools.partial(weight_kernel, groups, outs),
            [((1, units, width), BF16)] * outs,
            (at, own, *mine, *others, factor, *across(factor)),
            smem=1,
            scratch=[pltpu.VMEM((groups, capacity, width), BF16)],
            flops=outs * product,
            moved=5 * 10**6,
        )

    (d_w_down,) = weight_grads(own_grad, sent_grad, weighed, 1)
    d_w_gate, d_w_up = weight_grads(own_in, sent_in, grads, 2)
    return (d_tokens, d_combine[None], d_w_gate, d_w_up, d_w_down)


def solution(mesh):
    in_specs = (
        P(("grp", "exp"), None),
        P(("grp", "exp"), None),
        P(("grp", "exp")),
        P(),
        P(),
        P(),
        P("grp", None, None),
        P("grp", None, None),
        P("exp", None, None),
        P("exp", None, None),
        P("exp", None, None),
    )
    out_specs = (
        P(("grp", "exp"), None),
        P("grp", "exp", None),
        P("exp", None, "grp"),
        P("exp", None, "grp"),
        P("exp", None, "grp"),
    )
    return jax.shard_map(on_device, mesh=mesh, in_specs=in_specs, out_specs=out_specs, check_vma=False)
```

```python
import functools

import jax
import jax.numpy as jnp
from jax import lax
from jax.experimental import pallas as pl
from jax.experimental.pallas import tpu as pltpu
from jax.sharding import PartitionSpec as P


EPSILON = 1e-06
F32 = jnp.float32
BF16 = jnp.bfloat16
NN = (((1,), (0,)), ((), ()))
NT = (((1,), (1,)), ((), ()))
TN = (((0,), (0,)), ((), ()))


def dot(left, right, dims=NN):
    return lax.dot_general(left, right, dims, preferred_element_type=F32)


def swap(shard, axis, bits):
    return lax.ppermute(shard, axis, [(i, i ^ bits) for i in range(lax.axis_size(axis))])


def iota(shape, dim):
    return lax.broadcasted_iota(jnp.int32, shape, dim)


def call(body, outs, args, smem=0, scratch=(), flops=0, moved=0, grant=20):
    spaces = [pltpu.SMEM] * smem + [pltpu.VMEM] * (len(args) - smem)
    return pl.pallas_call(
        body,
        out_shape=[jax.ShapeDtypeStruct(shape, dtype) for shape, dtype in outs],
        in_specs=[pl.BlockSpec(memory_space=space) for space in spaces],
        out_specs=[pl.BlockSpec(memory_space=pltpu.VMEM) for _ in outs],
        scratch_shapes=list(scratch),
        cost_estimate=pl.CostEstimate(flops=flops, bytes_accessed=moved, transcendentals=0),
        compiler_params=pltpu.CompilerParams(vmem_limit_bytes=grant * 2**20),
    )(*args)


def table_rows(step_ref, table):
    classes = table.shape[0]
    tokens = step_ref.shape[1]
    picks = (iota((classes, tokens), 0) == step_ref[...]).astype(F32).T.astype(BF16)
    high = table.astype(BF16)
    rest = table - high.astype(F32)
    middle = rest.astype(BF16)
    low = (rest - middle.astype(F32)).astype(BF16)
    return dot(picks, high) + dot(picks, middle) + dot(picks, low)


def layer_stats(values):
    centred = values - jnp.mean(values, axis=1, keepdims=True)
    inverse = lax.rsqrt(jnp.mean(centred * centred, axis=1, keepdims=True) + EPSILON)
    return centred * inverse, inverse


def pick_kernel(slots, at_ref, tokens_ref, step_ref, shift_ref, scale_ref, chosen_ref, pick_ref, *out_refs):
    experts, capacity = chosen_ref.shape
    count = tokens_ref.shape[0]
    device = at_ref[0]
    here = device // 2
    ones = jnp.ones((8, capacity), BF16)
    earlier = (iota((count, count), 0) < iota((count, count), 1)).astype(BF16)
    for j in range(experts):
        wanted = chosen_ref[pl.ds(here ^ j, 1), :] - device * count
        named = (iota((count, capacity), 0) == wanted).astype(F32).astype(BF16)
        taken = dot(ones, named, NT)
        place = dot(taken.astype(BF16), earlier)
        match = (place[0:1].astype(jnp.int32) == iota((slots, count), 0)) & (taken[0:1] > 0.5)
        pick_ref[j * slots : (j + 1) * slots, :] = match.astype(F32).astype(BF16)
    normed, _ = layer_stats(tokens_ref[...].astype(F32))
    scale = table_rows(step_ref, scale_ref[...])
    shift = table_rows(step_ref, shift_ref[...])
    modulated = (normed * (1.0 + scale) + shift).astype(BF16)
    for j in range(experts):
        out_refs[j][...] = dot(pick_ref[j * slots : (j + 1) * slots, :], modulated).astype(BF16)


def grad_kernel(slots, cotangent_ref, step_ref, gate_ref, pick_ref, *out_refs):
    gate = table_rows(step_ref, gate_ref[...])
    scaled = (gate * cotangent_ref[...].astype(F32)).astype(BF16)
    for j in range(len(out_refs)):
        out_refs[j][...] = dot(pick_ref[j * slots : (j + 1) * slots, :], scaled).astype(BF16)


def place_kernel(count, slots, at_ref, chosen_ref, place_ref, back_ref):
    experts, capacity = chosen_ref.shape
    device = at_ref[0]
    here, core = device // 2, device % 2
    shift = count.bit_length() - 1
    row = chosen_ref[pl.ds(here, 1), :]
    across = jnp.broadcast_to(row, (capacity, capacity))
    down = across.astype(F32).T.astype(jnp.int32)

    def slot_of(tokens, ranks):
        owner = lax.shift_right_logical(tokens, shift)
        apart = lax.shift_right_logical(owner, 1) ^ here
        other = (owner & 1) ^ core
        return (other * experts + apart) * slots + ranks

    owner_across = lax.shift_right_logical(across, shift)
    owner_down = lax.shift_right_logical(down, shift)
    same = owner_across == owner_down
    rank_down = jnp.sum((same & (across < down)).astype(F32), axis=1, keepdims=True)
    rank_across = jnp.sum((same & (down < across)).astype(F32), axis=0, keepdims=True)
    slot_down = slot_of(down[:, 0:1], rank_down.astype(jnp.int32))
    slot_across = slot_of(row, rank_across.astype(jnp.int32))
    total = place_ref.shape[1]
    place_ref[...] = (iota((capacity, total), 1) == slot_down).astype(F32).astype(BF16)
    back_ref[...] = (iota((total, capacity), 0) == slot_across).astype(F32).astype(BF16)


def gather_rows(place_ref, block_refs, slot_ref):
    slots = block_refs[0].shape[0]
    for index, block in enumerate(block_refs):
        slot_ref[index * slots : (index + 1) * slots, :] = block[...]
    return dot(place_ref[...], slot_ref[...]).astype(BF16)


def put_slices(rows_ref, at_ref, own_ref, sent_refs):
    half = rows_ref.shape[0] // 2
    width = own_ref.shape[1]
    core, group = at_ref[0] % 2, at_ref[1]
    mine = pl.ds(pl.multiple_of(core * half, half), half)
    own_ref[...] = rows_ref[:, pl.ds(pl.multiple_of(group * width, width), width)]
    for j, sent in enumerate(sent_refs):
        start = pl.multiple_of((group ^ (j + 1)) * width, width)
        sent[...] = rows_ref[mine, pl.ds(start, width)]


def forward_kernel(blocks, groups, at_ref, *refs):
    block_refs = refs[:blocks]
    place_ref, combine_ref, gate_ref, up_ref = refs[blocks : blocks + 4]
    weighed_ref, pre_gate_ref, pre_up_ref, own_ref = refs[blocks + 4 : blocks + 8]
    sent_refs = refs[blocks + 8 : blocks + 7 + groups]
    slot_ref, rows_ref = refs[blocks + 7 + groups :]
    rows_ref[...] = gather_rows(place_ref, block_refs, slot_ref)
    put_slices(rows_ref, at_ref, own_ref, sent_refs)
    weight = combine_ref[pl.ds(at_ref[0] // 2, 1), :]
    pre_gate = dot(gate_ref[...], rows_ref[...], NT)
    pre_up = dot(up_ref[...], rows_ref[...], NT)
    weighed_ref[...] = (weight * (pre_gate * jax.nn.sigmoid(pre_gate) * pre_up)).astype(BF16)
    pre_gate_ref[...] = pre_gate
    pre_up_ref[...] = pre_up


def derive_kernel(at_ref, combine_ref, pre_gate_ref, pre_up_ref, hidden_ref, into_gate_ref, into_up_ref):
    weight = combine_ref[pl.ds(at_ref[0] // 2, 1), :]
    pre_gate, pre_up = pre_gate_ref[...], pre_up_ref[...]
    sigmoid = jax.nn.sigmoid(pre_gate)
    silu = pre_gate * sigmoid
    hidden_ref[...] = silu * pre_up
    into_gate_ref[...] = weight * pre_up * sigmoid * (1.0 + pre_gate * (1.0 - sigmoid))
    into_up_ref[...] = weight * silu


def backward_kernel(blocks, groups, at_ref, *refs):
    block_refs = refs[:blocks]
    place_ref, down_ref, hidden_ref, into_gate_ref, into_up_ref = refs[blocks : blocks + 5]
    grads_ref, inner_ref, own_ref = refs[blocks + 5 : blocks + 8]
    sent_refs = refs[blocks + 8 : blocks + 7 + groups]
    slot_ref, rows_ref = refs[blocks + 7 + groups :]
    half_units = down_ref.shape[0]
    rows_ref[...] = gather_rows(place_ref, block_refs, slot_ref)
    put_slices(rows_ref, at_ref, own_ref, sent_refs)
    raw = dot(down_ref[...], rows_ref[...], NT)
    grads_ref[:half_units, :] = (raw * into_gate_ref[...]).astype(BF16)
    grads_ref[half_units:, :] = (raw * into_up_ref[...]).astype(BF16)
    inner_ref[...] = jnp.sum(raw * hidden_ref[...], axis=0, keepdims=True)


def rows_kernel(grads_ref, gate_ref, up_ref, back_ref, rows_ref, other_ref):
    half_units = gate_ref.shape[0]
    total = dot(grads_ref[:half_units, :], gate_ref[...], TN)
    total += dot(grads_ref[half_units:, :], up_ref[...], TN)
    rows_ref[...] = total.astype(BF16)
    other_ref[...] = dot(back_ref[other_ref.shape[0] :, :], rows_ref[...]).astype(BF16)


def pair_kernel(rows_ref, back_ref, other_ref, *out_refs):
    slots = out_refs[0].shape[0]
    for j, out in enumerate(out_refs):
        at = slice(j * slots, (j + 1) * slots)
        out[...] = (dot(back_ref[at, :], rows_ref[...]) + other_ref[at, :].astype(F32)).astype(BF16)


def combine_kernel(at_ref, inner_ref, other_ref, out_ref):
    half = out_ref.shape[1]
    start = pl.ds(pl.multiple_of((at_ref[0] % 2) * half, half), half)
    out_ref[...] = inner_ref[:, start] + other_ref[:, start]


def final_kernel(tokens_ref, step_ref, scale_ref, pick_ref, *refs):
    block_refs, (out_ref, slot_ref) = refs[:-2], refs[-2:]
    slots = block_refs[0].shape[0]
    for j, block in enumerate(block_refs):
        slot_ref[j * slots : (j + 1) * slots, :] = block[...]
    d_modulated = dot(pick_ref[...], slot_ref[...], TN)
    normed, inverse = layer_stats(tokens_ref[...].astype(F32))
    d_normed = d_modulated * (1.0 + table_rows(step_ref, scale_ref[...]))
    out_ref[...] = (
        inverse
        * (
            d_normed
            - jnp.mean(d_normed, axis=1, keepdims=True)
            - normed * jnp.mean(d_normed * normed, axis=1, keepdims=True)
        )
    ).astype(BF16)


def weight_kernel(groups, outs, at_ref, *refs):
    own_ref = refs[0]
    mine_refs = refs[1:groups]
    other_refs = refs[groups : 2 * groups - 1]
    factor_refs = refs[2 * groups - 1 : 3 * groups - 1]
    out_refs = refs[3 * groups - 1 : 3 * groups - 1 + outs]
    rows_ref = refs[-1]
    capacity = own_ref.shape[0]
    half = capacity // 2
    core = at_ref[0] % 2
    rows_ref[0] = own_ref[...]
    for j in range(groups - 1):
        rows_ref[j + 1, pl.ds(pl.multiple_of(core * half, half), half), :] = mine_refs[j][...]
        rows_ref[j + 1, pl.ds(pl.multiple_of((1 - core) * half, half), half), :] = other_refs[j][...]
    units = out_refs[0].shape[1]
    for index, out in enumerate(out_refs):
        total = None
        for j in range(groups):
            part = dot(factor_refs[j][index * units : (index + 1) * units, :], rows_ref[j])
            total = part if total is None else total + part
        out[0] = (total / groups).astype(BF16)


def on_device(tokens, cotangent, timestep, shift_table, scale_table, gate_table, chosen, combine, w_gate, w_up, w_down):
    peers = lax.axis_size("exp")
    groups = lax.axis_size("grp")
    count, features = tokens.shape
    capacity = chosen.shape[2]
    experts = peers // 2
    slots = 2 * capacity // peers
    units = w_gate.shape[1]
    width = features // groups
    at = jnp.stack([lax.axis_index("exp"), lax.axis_index("grp")]).astype(jnp.int32)
    steps = timestep.reshape(1, count)
    lists, weights = chosen[0], combine[0]
    gate_half, up_half, down_half = w_gate[0], w_up[0], w_down[0]
    sent = [((slots, features), BF16)] * experts
    product = 2 * capacity * features * units

    def dispatch(parts):
        arrived = [parts[0]] + [swap(parts[j], "exp", 2 * j) for j in range(1, experts)]
        return arrived + [swap(part, "exp", 1) for part in arrived]

    picks, *rows_out = call(
        functools.partial(pick_kernel, slots),
        [((experts * slots, count), BF16)] + sent,
        (at, tokens, steps, shift_table, scale_table, lists),
        smem=1,
        flops=10**9,
        moved=2 * 10**6,
    )
    blocks_in = dispatch(rows_out)
    grads_out = call(
        functools.partial(grad_kernel, slots), sent, (cotangent, steps, gate_table, picks), flops=10**9, moved=2 * 10**6
    )
    blocks_grad = dispatch(grads_out)
    place, back = call(
        functools.partial(place_kernel, count, slots),
        [((capacity, peers * slots), BF16), ((peers * slots, capacity), BF16)],
        (at, lists),
        smem=1,
        flops=10**8,
        moved=10**6,
    )
    slices = [((capacity, width), BF16)] + [((capacity // 2, width), BF16)] * (groups - 1)
    gather_scratch = [pltpu.VMEM((peers * slots, features), BF16), pltpu.VMEM((capacity, features), BF16)]
    wide = [((units, capacity), F32)]
    weighed, pre_gate, pre_up, own_in, *sent_in = call(
        functools.partial(forward_kernel, peers, groups),
        [((units, capacity), BF16)] + wide * 2 + slices,
        (at, *blocks_in, place, weights, gate_half, up_half),
        smem=1,
        scratch=gather_scratch,
        flops=3 * product,
        moved=12 * 10**6,
    )
    hidden, into_gate, into_up = call(
        derive_kernel, wide * 3, (at, weights, pre_gate, pre_up), smem=1, flops=10**7, moved=4 * 10**6
    )
    grads, inner, own_grad, *sent_grad = call(
        functools.partial(backward_kernel, peers, groups),
        [((2 * units, capacity), BF16), ((1, capacity), F32)] + slices,
        (at, *blocks_grad, place, down_half, hidden, into_gate, into_up),
        smem=1,
        scratch=gather_scratch,
        flops=2 * product,
        moved=10 * 10**6,
    )
    d_rows, d_other = call(
        rows_kernel,
        [((capacity, features), BF16), ((capacity, features), BF16)],
        (grads, gate_half, up_half, back),
        flops=3 * product,
        moved=10 * 10**6,
    )
    d_out = call(pair_kernel, sent, (d_rows, back, swap(d_other, "exp", 1)), flops=product // 2, moved=4 * 10**6)
    (d_combine,) = call(combine_kernel, [((1, capacity // 2), F32)], (at, inner, swap(inner, "exp", 1)), smem=1)
    returned = [d_out[0]] + [swap(d_out[j], "exp", 2 * j) for j in range(1, experts)]
    (d_tokens,) = call(
        final_kernel,
        [((count, features), BF16)],
        (tokens, steps, scale_table, picks, *returned),
        scratch=[pltpu.VMEM((experts * slots, features), BF16)],
        flops=10**9,
        moved=2 * 10**6,
    )

    def across(part):
        return [swap(part, "grp", j) for j in range(1, groups)]

    def weight_grads(own, sends, factors, outs):
        mine = [swap(part, "grp", j + 1) for j, part in enumerate(sends)]
        others = [swap(part, "exp", 1) for part in mine]
        return call(
            functools.partial(weight_kernel, groups, outs),
            [((1, units, width), BF16)] * outs,
            (at, own, *mine, *others, *factors),
            smem=1,
            scratch=[pltpu.VMEM((groups, capacity, width), BF16)],
            flops=outs * product,
            moved=5 * 10**6,
        )

    (d_w_down,) = weight_grads(own_grad, sent_grad, [weighed] + across(weighed), 1)
    d_w_gate, d_w_up = weight_grads(own_in, sent_in, [grads] + across(grads), 2)
    return (d_tokens, d_combine[None], d_w_gate, d_w_up, d_w_down)


def solution(mesh):
    in_specs = (
        P(("grp", "exp"), None),
        P(("grp", "exp"), None),
        P(("grp", "exp")),
        P(),
        P(),
        P(),
        P("grp", None, None),
        P("grp", None, None),
        P("exp", None, None),
        P("exp", None, None),
        P("exp", None, None),
    )
    out_specs = (
        P(("grp", "exp"), None),
        P("grp", "exp", None),
        P("exp", None, "grp"),
        P("exp", None, "grp"),
        P("exp", None, "grp"),
    )

    return jax.shard_map(on_device, mesh=mesh, in_specs=in_specs, out_specs=out_specs, check_vma=False)
```
